256 devices in a mesh: ctx: 64 (over z, x, y_hi), ch: 4 (over y_lo, core).
Axes of the slice: x: 4, y: 4 (y_hi: 2, y_lo: 2; y = y_hi * 2 + y_lo), z: 8, core: 2. Of those that a mesh axis runs over, the one named last changes fastest.
Arguments:
- query: bfloat16 [8192, 8192], P('ctx', 'ch'), may hold values from -6 to 6
- key: bfloat16 [8192, 8192], P('ctx', 'ch'), may hold values from -6 to 6
- value: bfloat16 [8192, 8192], P('ctx', 'ch'), may hold values from -6 to 6
- filter_taps: bfloat16 [1024, 512], P('ctx', 'ch'), may hold values from -0.1875 to 0.1875
- skip: float32 [8192], P('ch'), may hold values from -1 to 1
Outputs:
- gated: bfloat16 [8192, 8192], P('ctx', 'ch')
The draws below stay inside these ranges and needn't reach their ends.
All inputs are finite; a program needn't handle non-finite values.
Results may differ from the reference program's by a relative error of at most 0.0085.
Values may be sent and summed in bfloat16 or wider, within the bound.
A program may use at most 192 MiB of HBM per device.

```python
import jax
import jax.numpy as jnp

D = 8192
GROUP = 16
BLOCK = 128
LAGS = 8
TAPS = 1024
GROUPS = 512
LENGTH = 8192


def level_of(key, shape, cuts, smallest, largest):
    def one(position, shards_of):
        steps = jax.random.uniform(jax.random.fold_in(jax.random.fold_in(key, 6), position), (shards_of,), jnp.float32, smallest / len(cuts), largest / len(cuts))
        return jnp.repeat(jnp.exp(steps), shape[position] // shards_of).reshape((-1,) + (1,) * (len(shape) - position - 1))

    loudness = one(*cuts[0])
    for cut in cuts[1:]:
        loudness = loudness * one(*cut)
    return loudness


def scatter_about(key, extent, spread, reach, split=(), held_as=jnp.bfloat16):
    entries = spread * jax.random.normal(key, extent, jnp.float32)
    if split:
        entries = entries * level_of(key, extent, split, -0.22, 0.18)
    return jnp.clip(entries, -reach, reach).astype(held_as)


def setup_inputs(seed: int = 0) -> dict:
    keys = jax.random.split(jax.random.key(seed), 6)
    return {
        "query": scatter_about(keys[0], (LENGTH, D), 1.0, 6.0, ((0, 64), (1, 4))),
        "key": scatter_about(keys[1], (LENGTH, D), 1.0, 6.0, ((0, 64), (1, 4))),
        "value": scatter_about(keys[2], (LENGTH, D), 1.0, 6.0, ((0, 64), (1, 4))),
        "filter_taps": scatter_about(keys[3], (TAPS, GROUPS), TAPS ** -0.5, 0.1875, ((0, 64), (1, 4))),
        "skip": jnp.clip(jax.random.uniform(keys[4], (D,), jnp.float32, -1.0, 1.0) * level_of(keys[4], (D,), ((0, 4),), -0.4, 0.0), -1.0, 1.0),
    }


def reference(query, key, value, filter_taps, skip):
    length = query.shape[0]
    channels = query.shape[1]
    groups = channels // GROUP
    nblocks = length // BLOCK
    mixed = (key.astype(jnp.float32) * value.astype(jnp.float32)).astype(jnp.bfloat16)
    blocks = mixed.astype(jnp.float32).reshape(nblocks, BLOCK, groups, GROUP)
    taps_float = filter_taps.astype(jnp.float32).T
    padded = jnp.concatenate([jnp.zeros((groups, BLOCK), jnp.float32), taps_float, jnp.zeros((groups, BLOCK), jnp.float32)], axis=1)
    offsets = (BLOCK - 1) + jnp.arange(BLOCK)[:, None] - jnp.arange(BLOCK)[None, :]
    summed = jnp.zeros((nblocks, BLOCK, groups, GROUP), jnp.float32)
    for lag_index in range(LAGS):
        window = padded[:, lag_index * BLOCK + 1: lag_index * BLOCK + 1 + 2 * BLOCK]
        toeplitz = window[:, offsets]
        earlier = jnp.concatenate([jnp.zeros((lag_index, BLOCK, groups, GROUP), jnp.float32), blocks[:nblocks - lag_index]], axis=0)
        summed = summed + jnp.einsum('gts,nsgc->ntgc', toeplitz, earlier)
    conv = summed.reshape(length, channels)
    gated = query.astype(jnp.float32) * (conv + skip[None, :] * mixed.astype(jnp.float32))
    return gated.astype(jnp.bfloat16)
```

```python
import functools

import jax
import jax.numpy as jnp
from jax import lax
from jax.experimental import pallas as pl
from jax.experimental.pallas import tpu as pltpu
from jax.sharding import PartitionSpec as P

MESH = pl.DeviceIdType.MESH
GROUP = 16
BLOCK = 128
LAGS = 8
PLANE = 8
CHUNKS = 2


def kernel(planes, q_hbm, k_hbm, v_hbm, taps_hbm, skip_hbm, out_ref,
           q_v, k_v, v_v, skip_v, skip_rows, mixed, source, taps_in, taps_f, taps_own, taps_all, taps_row,
           toeplitz, result, back,
           load_sem, tap_send, tap_recv, line_send, line_recv, credit,
           own_send, own_recv, halo_send, halo_recv, back_send, back_recv):
    ctx, ch = lax.axis_index("ctx"), lax.axis_index("ch")
    z, me = ctx // PLANE, ctx % PLANE
    last = planes - 1
    groups = source.shape[0]
    part = groups // CHUNKS

    def at(plane, place):
        return (plane * PLANE + place, ch)

    def remote(src, dst, send, recv, device):
        return pltpu.make_async_remote_copy(
            src_ref=src, dst_ref=dst, send_sem=send, recv_sem=recv,
            device_id=device, device_id_type=MESH)

    barrier = pltpu.get_barrier_semaphore()
    for step in range(1, PLANE):
        pl.semaphore_signal(barrier, inc=1, device_id=at(z, (me + step) % PLANE), device_id_type=MESH)

    @pl.when(z > 0)
    def _():
        for step in range(PLANE):
            pl.semaphore_signal(barrier, inc=1, device_id=at(z - 1, (me + step) % PLANE), device_id_type=MESH)

    for step in range(1, planes):
        @pl.when(z + step < planes)
        def _(step=step):
            pl.semaphore_signal(barrier, inc=1, device_id=at(z + step, me), device_id_type=MESH)

    loads = [
        pltpu.make_async_copy(k_hbm, k_v, load_sem.at[0]),
        pltpu.make_async_copy(v_hbm, v_v, load_sem.at[1]),
        pltpu.make_async_copy(taps_hbm, taps_in.at[me], load_sem.at[2]),
        pltpu.make_async_copy(skip_hbm.at[pl.ds(pl.multiple_of(me * groups * GROUP, 256), groups * GROUP)], skip_v, load_sem.at[3]),
        pltpu.make_async_copy(q_hbm, q_v, load_sem.at[4]),
    ]
    for load in loads:
        load.start()

    @pl.when(z == 0)
    def _():
        source[:, 0:LAGS - 1] = jnp.zeros((groups, LAGS - 1, GROUP, BLOCK), jnp.bfloat16)

    pl.semaphore_wait(barrier, PLANE - 1 + z + jnp.where(z < last, PLANE, 0))

    tap_copies = []
    for step in range(1, PLANE):
        copy = remote(taps_hbm, taps_in.at[me], tap_send, tap_recv, at(z, (me + step) % PLANE))
        copy.start()
        tap_copies.append(copy)

    loads[0].wait()
    loads[1].wait()
    own_copies = []
    local_copies = []
    halo_copies = []
    for chunk in range(CHUNKS):
        rows = pl.ds(chunk * part, part)
        for step in range(1, PLANE + 1):
            to = (me + step) % PLANE
            width = part * GROUP
            lanes = pl.ds(pl.multiple_of(to * groups * GROUP + chunk * width, width), width)
            m = (k_v[:, lanes].astype(jnp.float32) * v_v[:, lanes].astype(jnp.float32))
            m = m.T.astype(jnp.bfloat16).reshape(part, GROUP, BLOCK)
            mixed[to, rows] = m
            if step < PLANE:
                copy = remote(mixed.at[to, rows], source.at[rows, LAGS - 1 + me], own_send, own_recv.at[chunk], at(z, to))
                copy.start()
                own_copies.append(copy)
            else:
                copy = pltpu.make_async_copy(mixed.at[to, rows], source.at[rows, LAGS - 1 + me], load_sem.at[5 + chunk])
                copy.start()
                local_copies.append(copy)

            @pl.when((z < last) & (me > 0))
            def _(to=to, rows=rows, chunk=chunk):
                remote(mixed.at[to, rows], source.at[rows, jnp.maximum(me - 1, 0)], halo_send, halo_recv.at[chunk],
                       at(jnp.minimum(z + 1, last), to)).start()

    loads[2].wait()
    pltpu.make_async_copy(taps_in.at[0:PLANE - 1], taps_in.at[0:PLANE - 1], tap_recv).wait()
    taps_f[...] = taps_in[...].astype(jnp.float32).reshape(BLOCK, BLOCK).T
    taps_own[...] = taps_f[pl.ds(pl.multiple_of(me * groups, groups), groups), :].astype(jnp.bfloat16)

    def line(step):
        return remote(taps_own, taps_all.at[z], line_send, line_recv, at(jnp.clip(z + step, 0, last), me))

    for step in range(-last, 2):
        if step != 0:
            @pl.when((z + step >= 0) & (z + step <= last))
            def _(step=step):
                line(step).start()
    for step in range(2, planes):
        @pl.when(z - step >= 0)
        def _(step=step):
            pl.semaphore_signal(credit, inc=1, device_id=at(z - step, me), device_id_type=MESH)

    @pl.when(z < last - 1)
    def _():
        pl.semaphore_wait(credit, last - 1 - z)

    for step in range(2, planes):
        @pl.when(z + step <= last)
        def _(step=step):
            line(step).start()
    taps_all[z] = taps_own[...]

    pltpu.make_async_copy(taps_all.at[0:planes - 1], taps_all.at[0:planes - 1], line_recv).wait()

    taps_row[...] = taps_all[...].astype(jnp.float32)
    u = lax.broadcasted_iota(jnp.int32, (BLOCK, BLOCK), 0)
    t = lax.broadcasted_iota(jnp.int32, (BLOCK, BLOCK), 1)
    reached = t >= u

    @pl.loop(0, groups)
    def _(g):
        before = jnp.zeros((BLOCK, BLOCK), jnp.float32)
        for lag in range(LAGS):
            row = taps_row[lag, pl.ds(g, 1), :]
            turned = pltpu.roll(jnp.broadcast_to(row, (BLOCK, BLOCK)), 0, 1, stride=1, stride_axis=0)
            toeplitz[g, lag * BLOCK:(lag + 1) * BLOCK, :] = jnp.where(reached, turned, before).astype(jnp.bfloat16)
            before = turned

    loads[3].wait()
    for half in range(groups * GROUP // BLOCK):
        row = skip_v[half * BLOCK:(half + 1) * BLOCK].reshape(1, BLOCK)
        per = BLOCK // GROUP
        skip_rows[half * per:(half + 1) * per] = jnp.broadcast_to(row, (BLOCK, BLOCK)).T.reshape(per, GROUP, BLOCK)

    for copy in local_copies:
        copy.wait()
    back_copies = []
    for chunk in range(CHUNKS):
        rows = pl.ds(chunk * part, part)
        landed = mixed.at[0:PLANE - 1, rows]
        pltpu.make_async_copy(landed, landed, own_recv.at[chunk]).wait()

        @pl.when(z > 0)
        def _(landed=landed, chunk=chunk):
            pltpu.make_async_copy(landed, landed, halo_recv.at[chunk]).wait()

        @pl.loop(chunk * part, (chunk + 1) * part)
        def _(g):
            total = jnp.broadcast_to(skip_rows[g][None], (PLANE, GROUP, BLOCK)).reshape(BLOCK, BLOCK)
            total = total * source[g, LAGS - 1:LAGS - 1 + PLANE].reshape(BLOCK, BLOCK).astype(jnp.float32)
            for lag in range(0, LAGS, 2):
                here = source[g, LAGS - 1 - lag:LAGS - 1 - lag + PLANE].reshape(BLOCK, BLOCK)
                there = source[g, LAGS - 2 - lag:LAGS - 2 - lag + PLANE].reshape(BLOCK, BLOCK)
                total = total + jnp.dot(
                    jnp.concatenate([here, there], axis=1),
                    toeplitz[g, lag * BLOCK:(lag + 2) * BLOCK, :],
                    preferred_element_type=jnp.float32)
            result[:, g] = total.astype(jnp.bfloat16).reshape(PLANE, GROUP, BLOCK)

        for step in range(1, PLANE + 1):
            to = (me + step) % PLANE
            if step < PLANE:
                copy = remote(result.at[to, rows], back.at[me, rows], back_send, back_recv.at[chunk], at(z, to))
                copy.start()
                back_copies.append(copy)
            else:
                back[me, rows] = result[me, rows]

    loads[4].wait()
    for chunk in range(CHUNKS):
        rows = pl.ds(chunk * part, part)
        landed = mixed.at[0:PLANE - 1, rows]
        pltpu.make_async_copy(landed, landed, back_recv.at[chunk]).wait()
        for place in range(PLANE):
            width = part * GROUP
            first = place * groups * GROUP + chunk * width
            lanes = slice(first, first + width)
            turned = back[place, rows].reshape(width, BLOCK).astype(jnp.float32).T
            out_ref[:, lanes] = (q_v[:, lanes].astype(jnp.float32) * turned).astype(jnp.bfloat16)

    for copy in tap_copies + own_copies + back_copies:
        copy.wait_send()
    for step in range(1, planes):
        line(1).wait_send()

    @pl.when((z < last) & (me > 0))
    def _():
        for chunk in range(CHUNKS):
            rows = pl.ds(chunk * part, part)
            for _ in range(PLANE):
                remote(mixed.at[0, rows], source.at[rows, 0], halo_send, halo_recv.at[chunk], at(z, me)).wait_send()


def solution(mesh):
    planes = mesh.shape["ctx"] // PLANE

    def per_device(query, key, value, filter_taps, skip):
        tokens, channels = query.shape
        groups = channels // GROUP // PLANE
        hbm = pl.BlockSpec(memory_space=pl.ANY)
        bf16, f32 = jnp.bfloat16, jnp.float32
        dma = pltpu.SemaphoreType.DMA
        return pl.pallas_call(
            functools.partial(kernel, planes),
            out_shape=jax.ShapeDtypeStruct((tokens, channels), bf16),
            in_specs=[hbm] * 5,
            out_specs=pl.BlockSpec(memory_space=pltpu.VMEM),
            scratch_shapes=[
                pltpu.VMEM((tokens, channels), bf16),
                pltpu.VMEM((tokens, channels), bf16),
                pltpu.VMEM((tokens, channels), bf16),
                pltpu.VMEM((groups * GROUP,), f32),
                pltpu.VMEM((groups, GROUP, BLOCK), f32),
                pltpu.VMEM((PLANE, groups, GROUP, BLOCK), bf16),
                pltpu.VMEM((groups, LAGS - 1 + PLANE, GROUP, BLOCK), bf16),
                pltpu.VMEM((PLANE, BLOCK // PLANE, BLOCK), bf16),
                pltpu.VMEM((BLOCK, BLOCK), f32),
                pltpu.VMEM((groups, BLOCK), bf16),
                pltpu.VMEM((planes, groups, BLOCK), bf16),
                pltpu.VMEM((planes, groups, BLOCK), f32),
                pltpu.VMEM((groups, LAGS * BLOCK, BLOCK), bf16),
                pltpu.VMEM((PLANE, groups, GROUP, BLOCK), bf16),
                pltpu.VMEM((PLANE, groups, GROUP, BLOCK), bf16),
                dma((5 + CHUNKS,)),
                dma, dma, dma, dma,
                pltpu.SemaphoreType.REGULAR,
                dma, dma((CHUNKS,)), dma, dma((CHUNKS,)), dma, dma((CHUNKS,)),
            ],
            compiler_params=pltpu.CompilerParams(collective_id=0, has_side_effects=True, vmem_limit_bytes=48 << 20),
        )(query, key, value, filter_taps, skip)

    placed = (P("ctx", "ch"), P("ctx", "ch"), P("ctx", "ch"), P("ctx", "ch"), P("ch"))
    return jax.shard_map(per_device, mesh=mesh, in_specs=placed, out_specs=P("ctx", "ch"), check_vma=False)
```

```python
import functools

import jax
import jax.numpy as jnp
from jax import lax
from jax.experimental import pallas as pl
from jax.experimental.pallas import tpu as pltpu
from jax.sharding import PartitionSpec as P

MESH = pl.DeviceIdType.MESH
GROUP = 16
BLOCK = 128
LAGS = 8
PLANE = 8
ORDER = (0, 1)
DIRECT = (0, 1)
STEPS = 2
CHUNKS = 4


def kernel(planes, k_hbm, v_hbm, taps_hbm, skip_hbm, back,
           k_v, v_v, skip_v, skip_rows, mixed, source, taps_in, taps_f, taps_own, taps_all, taps_row,
           toeplitz, result,
           load_sem, local_sem, tap_send, tap_recv, line_send, line_recv, credit,
           own_send, own_recv, halo_send, halo_recv, back_send, back_recv):
    ctx, ch = lax.axis_index("ctx"), lax.axis_index("ch")
    z, me = ctx // PLANE, ctx % PLANE
    last = planes - 1
    groups = source.shape[0]
    half = groups // 2
    width = half * GROUP
    part = groups // CHUNKS
    f32, bf16 = jnp.float32, jnp.bfloat16

    def at(plane, place):
        return (plane * PLANE + place, ch)

    def remote(src, dst, send, recv, device):
        return pltpu.make_async_remote_copy(
            src_ref=src, dst_ref=dst, send_sem=send, recv_sem=recv,
            device_id=device, device_id_type=MESH)

    barrier = pltpu.get_barrier_semaphore()
    for step in range(1, PLANE):
        pl.semaphore_signal(barrier, inc=1, device_id=at(z, (me + step) % PLANE), device_id_type=MESH)

    @pl.when(z > 0)
    def _():
        for step in range(PLANE):
            pl.semaphore_signal(barrier, inc=1, device_id=at(z - 1, (me + step) % PLANE), device_id_type=MESH)

    for step in range(1, planes):
        @pl.when(z + step < planes)
        def _(step=step):
            pl.semaphore_signal(barrier, inc=1, device_id=at(z + step, me), device_id_type=MESH)

    loads = [
        pltpu.make_async_copy(k_hbm, k_v, load_sem.at[0]),
        pltpu.make_async_copy(v_hbm, v_v, load_sem.at[1]),
        pltpu.make_async_copy(taps_hbm, taps_in.at[me], load_sem.at[2]),
        pltpu.make_async_copy(skip_hbm.at[pl.ds(pl.multiple_of(me * groups * GROUP, 256), groups * GROUP)], skip_v, load_sem.at[3]),
    ]
    for load in loads:
        load.start()

    @pl.when(z == 0)
    def _():
        source[:, 0:LAGS - 1] = jnp.zeros((groups, LAGS - 1, GROUP, BLOCK), bf16)

    pl.semaphore_wait(barrier, PLANE - 1 + z + jnp.where(z < last, PLANE, 0))

    tap_copies = []
    for step in range(1, PLANE):
        copy = remote(taps_hbm, taps_in.at[me], tap_send, tap_recv, at(z, (me + step) % PLANE))
        copy.start()
        tap_copies.append(copy)

    for step in range(2, planes):
        @pl.when(z - step >= 0)
        def _(step=step):
            pl.semaphore_signal(credit, inc=1, device_id=at(z - step, me), device_id_type=MESH)

    loads[0].wait()
    loads[1].wait()
    own_copies = []
    local_copies = {}

    def halves(which):
        return pl.ds(which * half, half)

    def mix(to, which):
        lanes = pl.ds(pl.multiple_of(to * groups * GROUP + which * width, width), width)
        m = (k_v[:, lanes].astype(f32) * v_v[:, lanes].astype(f32)).T
        mixed[to, halves(which)] = m.astype(bf16).reshape(half, GROUP, BLOCK)

    def send_own(to, which):
        copy = remote(mixed.at[to, halves(which)], source.at[halves(which), LAGS - 1 + me], own_send, own_recv.at[which], at(z, to))
        copy.start()
        own_copies.append(copy)

    def keep_own(which):
        copy = pltpu.make_async_copy(mixed.at[me, halves(which)], source.at[halves(which), LAGS - 1 + me], local_sem.at[which])
        copy.start()
        local_copies[which] = copy

    def halo(to, which):
        return remote(mixed.at[to, halves(which)], source.at[halves(which), jnp.maximum(me - 1, 0)], halo_send.at[0], halo_recv.at[which],
                      at(jnp.minimum(z + 1, last), to))

    def forward(which):
        return remote(source.at[halves(which), LAGS:LAGS + PLANE - 1], source.at[halves(which), 0:LAGS - 1], halo_send.at[1],
                      halo_recv.at[which], at(jnp.minimum(z + 1, last), me))

    places = [(me + step) % PLANE for step in range(1, PLANE)] + [me]
    for which in ORDER:
        for to in places:
            mix(to, which)
            if to is not me:
                send_own(to, which)
            if which in DIRECT:
                @pl.when((z < last) & (me > 0))
                def _(to=to, which=which):
                    halo(to, which).start()
        keep_own(which)

    loads[2].wait()
    pltpu.make_async_copy(taps_in.at[0:PLANE - 1], taps_in.at[0:PLANE - 1], tap_recv).wait()
    taps_f[...] = taps_in[...].astype(f32).reshape(BLOCK, BLOCK).T
    taps_own[...] = taps_f[pl.ds(pl.multiple_of(me * groups, groups), groups), :].astype(bf16)

    def line(step):
        return remote(taps_own, taps_all.at[z], line_send, line_recv.at[z], at(jnp.clip(z + step, 0, last), me))

    for step in range(-last, 2):
        if step != 0:
            @pl.when((z + step >= 0) & (z + step <= last))
            def _(step=step):
                line(step).start()
    taps_all[z] = taps_own[...]

    loads[3].wait()
    per = BLOCK // GROUP
    for piece in range(groups // per):
        row = skip_v[piece * BLOCK:(piece + 1) * BLOCK].reshape(1, BLOCK)
        skip_rows[piece * per:(piece + 1) * per] = jnp.broadcast_to(row, (BLOCK, BLOCK)).T.reshape(per, GROUP, BLOCK)

    landed = mixed.at[0:PLANE - 1, pl.ds(0, half)]

    def wait_own(which):
        local_copies[which].wait()
        pltpu.make_async_copy(landed, landed, own_recv.at[which]).wait()

    for which in ORDER:
        if which not in DIRECT:
            wait_own(which)

            @pl.when(z < last)
            def _(which=which):
                forward(which).start()

    @pl.when(z < last - 1)
    def _():
        pl.semaphore_wait(credit, last - 1 - z)

    for step in range(2, planes):
        @pl.when(z + step <= last)
        def _(step=step):
            line(step).start()

    u = lax.broadcasted_iota(jnp.int32, (BLOCK, BLOCK), 0)
    t = lax.broadcasted_iota(jnp.int32, (BLOCK, BLOCK), 1)
    reached = t >= u

    def turn(lag, g):
        row = taps_row[lag, pl.ds(g, 1), :]
        return pltpu.roll(jnp.broadcast_to(row, (BLOCK, BLOCK)), 0, 1, stride=1, stride_axis=0)

    def rows_of(lags):
        for lag in lags:
            @pl.when(z != lag)
            def _(lag=lag):
                pltpu.make_async_copy(taps_own, taps_own, line_recv.at[lag]).wait()
            taps_row[lag] = taps_all[lag].astype(f32)

    def build(lags, g):
        before = turn(lags[0] - 1, g) if lags[0] else jnp.zeros((BLOCK, BLOCK), f32)
        for lag in lags:
            turned = turn(lag, g)
            toeplitz[g, lag * BLOCK:(lag + 1) * BLOCK, :] = jnp.where(reached, turned, before).astype(bf16)
            before = turned

    early, late = range(0, LAGS // 2), range(LAGS // 2, LAGS)
    rows_of(early)

    @pl.loop(0, groups, unroll=2)
    def _(g):
        build(early, g)

    rows_of(late)

    back_copies = []
    for chunk in range(CHUNKS):
        rows = pl.ds(chunk * part, part)
        which = chunk * part // half
        if chunk * part % half == 0:
            if which in DIRECT:
                wait_own(which)

            @pl.when(z > 0)
            def _(which=which):
                pltpu.make_async_copy(landed, landed, halo_recv.at[which]).wait()

        @pl.loop(chunk * part, (chunk + 1) * part, unroll=part)
        def _(g):
            build(late, g)
            total = jnp.broadcast_to(skip_rows[g][None], (PLANE, GROUP, BLOCK)).reshape(BLOCK, BLOCK)
            total = total * source[g, LAGS - 1:LAGS - 1 + PLANE].reshape(BLOCK, BLOCK).astype(f32)
            windows = [source[g, LAGS - 1 - lag:LAGS - 1 - lag + PLANE].reshape(BLOCK, BLOCK) for lag in range(LAGS)]
            total = total + jnp.dot(jnp.concatenate(windows, axis=1), toeplitz[g], preferred_element_type=f32)
            result[:, g] = total.astype(bf16).reshape(PLANE, GROUP, BLOCK)

        for to in places[:-1]:
            copy = remote(result.at[to, rows], back.at[me, rows], back_send, back_recv, at(z, to))
            copy.start()
            back_copies.append(copy)
    home = pltpu.make_async_copy(result.at[me], back.at[me], local_sem.at[2])
    home.start()
    home.wait()

    for copy in tap_copies + own_copies + back_copies:
        copy.wait_send()
    for step in range(1, planes):
        line(1).wait_send()

    @pl.when((z < last) & (me > 0))
    def _():
        for which in DIRECT:
            for _ in range(PLANE):
                halo(me, which).wait_send()

    @pl.when(z < last)
    def _():
        for which in range(2):
            if which not in DIRECT:
                forward(which).wait_send()

    pltpu.make_async_copy(back.at[0:PLANE - 1], back.at[0:PLANE - 1], back_recv).wait()


def gate(back_ref, q_ref, out_ref):
    for first in range(0, q_ref.shape[1], BLOCK):
        lanes = slice(first, first + BLOCK)
        turned = back_ref[lanes, :].astype(jnp.float32).T
        out_ref[:, lanes] = (q_ref[:, lanes].astype(jnp.float32) * turned).astype(jnp.bfloat16)


def solution(mesh):
    planes = mesh.shape["ctx"] // PLANE

    def per_device(query, key, value, filter_taps, skip):
        tokens, channels = query.shape
        groups = channels // GROUP // PLANE
        hbm = pl.BlockSpec(memory_space=pl.ANY)
        bf16, f32 = jnp.bfloat16, jnp.float32
        dma = pltpu.SemaphoreType.DMA
        back = pl.pallas_call(
            functools.partial(kernel, planes),
            out_shape=jax.ShapeDtypeStruct((PLANE, groups, GROUP, BLOCK), bf16),
            in_specs=[hbm] * 4,
            out_specs=hbm,
            scratch_shapes=[
                pltpu.VMEM((tokens, channels), bf16),
                pltpu.VMEM((tokens, channels), bf16),
                pltpu.VMEM((groups * GROUP,), f32),
                pltpu.VMEM((groups, GROUP, BLOCK), f32),
                pltpu.VMEM((PLANE, groups, GROUP, BLOCK), bf16),
                pltpu.VMEM((groups, LAGS - 1 + PLANE, GROUP, BLOCK), bf16),
                pltpu.VMEM((PLANE, BLOCK // PLANE, BLOCK), bf16),
                pltpu.VMEM((BLOCK, BLOCK), f32),
                pltpu.VMEM((groups, BLOCK), bf16),
                pltpu.VMEM((planes, groups, BLOCK), bf16),
                pltpu.VMEM((planes, groups, BLOCK), f32),
                pltpu.VMEM((groups, LAGS * BLOCK, BLOCK), bf16),
                pltpu.VMEM((PLANE, groups, GROUP, BLOCK), bf16),
                dma((4,)), dma((3,)),
                dma, dma, dma, dma((planes,)),
                pltpu.SemaphoreType.REGULAR,
                dma, dma((2,)), dma((2,)), dma((2,)), dma, dma,
            ],
            compiler_params=pltpu.CompilerParams(collective_id=0, has_side_effects=True),
        )(key, value, filter_taps, skip)
        steps = STEPS
        return pl.pallas_call(
            gate,
            grid=(steps,),
            out_shape=jax.ShapeDtypeStruct((tokens, channels), bf16),
            in_specs=[pl.BlockSpec((channels // steps, BLOCK), lambda i: (i, 0)), pl.BlockSpec((tokens, channels // steps), lambda i: (0, i))],
            out_specs=pl.BlockSpec((tokens, channels // steps), lambda i: (0, i)),
        )(back.reshape(channels, BLOCK), query)

    placed = (P("ctx", "ch"), P("ctx", "ch"), P("ctx", "ch"), P("ctx", "ch"), P("ch"))
    return jax.shard_map(per_device, mesh=mesh, in_specs=placed, out_specs=P("ctx", "ch"), check_vma=False)
```

```python
import functools

import jax
import jax.numpy as jnp
from jax import lax
from jax.experimental import pallas as pl
from jax.experimental.pallas import tpu as pltpu
from jax.sharding import PartitionSpec as P

MESH = pl.DeviceIdType.MESH
GROUP = 16
BLOCK = 128
LAGS = 8
PLANE = 8
PLAN = ((('m', 0), ('m', 1), ('o', 3), ('o', 0), ('h', 0), ('h', 1)), (('h', 2), ('o', 1), ('o', 2)), (('f', 3),), ())
STEPS = 2
CHUNKS = 4


def kernel(planes, k_hbm, v_hbm, taps_hbm, skip_hbm, back,
           k_v, v_v, skip_v, skip_rows, mixed, source, taps_in, taps_f, taps_own, taps_all, taps_row,
           toeplitz, result,
           load_sem, local_sem, tap_send, tap_recv, line_send, line_recv, credit,
           own_send, own_recv, halo_send, halo_recv, back_send, back_recv):
    ctx, ch = lax.axis_index("ctx"), lax.axis_index("ch")
    z, me = ctx // PLANE, ctx % PLANE
    last = planes - 1
    groups = source.shape[0]
    half = groups // 2
    width = half * GROUP
    part = groups // CHUNKS
    f32, bf16 = jnp.float32, jnp.bfloat16

    def at(plane, place):
        return (plane * PLANE + place, ch)

    def remote(src, dst, send, recv, device):
        return pltpu.make_async_remote_copy(
            src_ref=src, dst_ref=dst, send_sem=send, recv_sem=recv,
            device_id=device, device_id_type=MESH)

    barrier = pltpu.get_barrier_semaphore()
    for step in range(1, PLANE):
        pl.semaphore_signal(barrier, inc=1, device_id=at(z, (me + step) % PLANE), device_id_type=MESH)

    @pl.when(z > 0)
    def _():
        for step in range(PLANE):
            pl.semaphore_signal(barrier, inc=1, device_id=at(z - 1, (me + step) % PLANE), device_id_type=MESH)

    for step in range(1, planes):
        @pl.when(z + step < planes)
        def _(step=step):
            pl.semaphore_signal(barrier, inc=1, device_id=at(z + step, me), device_id_type=MESH)

    loads = [
        pltpu.make_async_copy(k_hbm, k_v, load_sem.at[0]),
        pltpu.make_async_copy(v_hbm, v_v, load_sem.at[1]),
        pltpu.make_async_copy(taps_hbm, taps_in.at[me], load_sem.at[2]),
        pltpu.make_async_copy(skip_hbm.at[pl.ds(pl.multiple_of(me * groups * GROUP, 256), groups * GROUP)], skip_v, load_sem.at[3]),
    ]
    for load in loads:
        load.start()

    @pl.when(z == 0)
    def _():
        source[:, 0:LAGS - 1] = jnp.zeros((groups, LAGS - 1, GROUP, BLOCK), bf16)

    pl.semaphore_wait(barrier, PLANE - 1 + z + jnp.where(z < last, PLANE, 0))

    tap_copies = []
    for step in range(1, PLANE):
        copy = remote(taps_hbm, taps_in.at[me], tap_send, tap_recv, at(z, (me + step) % PLANE))
        copy.start()
        tap_copies.append(copy)

    for step in range(2, planes):
        @pl.when(z - step >= 0)
        def _(step=step):
            pl.semaphore_signal(credit, inc=1, device_id=at(z - step, me), device_id_type=MESH)

    loads[0].wait()
    loads[1].wait()
    own_copies = []
    local_copies = {}
    pieces = [pl.ds(chunk * part, part) for chunk in range(CHUNKS)]

    def mix(to, which):
        lanes = pl.ds(pl.multiple_of(to * groups * GROUP + which * width, width), width)
        m = (k_v[:, lanes].astype(f32) * v_v[:, lanes].astype(f32)).T
        mixed[to, pl.ds(which * half, half)] = m.astype(bf16).reshape(half, GROUP, BLOCK)

    def send_own(chunk):
        for to in places[:-1]:
            copy = remote(mixed.at[to, pieces[chunk]], source.at[pieces[chunk], LAGS - 1 + me], own_send, own_recv.at[chunk], at(z, to))
            copy.start()
            own_copies.append(copy)
        copy = pltpu.make_async_copy(mixed.at[me, pieces[chunk]], source.at[pieces[chunk], LAGS - 1 + me], local_sem.at[chunk])
        copy.start()
        local_copies[chunk] = copy

    def halo(to, chunk):
        return remote(mixed.at[to, pieces[chunk]], source.at[pieces[chunk], jnp.maximum(me - 1, 0)], halo_send.at[0], halo_recv.at[chunk],
                      at(jnp.minimum(z + 1, last), to))

    def send_halo(chunk):
        @pl.when((z < last) & (me > 0))
        def _():
            for to in places:
                halo(to, chunk).start()

    def forward(chunk):
        return remote(source.at[pieces[chunk], LAGS:LAGS + PLANE - 1], source.at[pieces[chunk], 0:LAGS - 1], halo_send.at[1],
                      halo_recv.at[chunk], at(jnp.minimum(z + 1, last), me))

    landed = mixed.at[0:PLANE - 1, pl.ds(0, part)]

    def wait_own(chunk):
        local_copies[chunk].wait()
        pltpu.make_async_copy(landed, landed, own_recv.at[chunk]).wait()

    def send_forward(chunk):
        wait_own(chunk)

        @pl.when(z < last)
        def _():
            forward(chunk).start()

    places = [(me + step) % PLANE for step in range(1, PLANE)] + [me]

    def run(stage):
        for what, which in stage:
            if what == "m":
                for to in places:
                    mix(to, which)
            if what == "o":
                send_own(which)
            if what == "h":
                send_halo(which)
            if what == "f":
                send_forward(which)

    run(PLAN[0])

    loads[2].wait()
    pltpu.make_async_copy(taps_in.at[0:PLANE - 1], taps_in.at[0:PLANE - 1], tap_recv).wait()
    taps_f[...] = taps_in[...].astype(f32).reshape(BLOCK, BLOCK).T
    taps_own[...] = taps_f[pl.ds(pl.multiple_of(me * groups, groups), groups), :].astype(bf16)

    def line(step):
        return remote(taps_own, taps_all.at[z], line_send, line_recv.at[z], at(jnp.clip(z + step, 0, last), me))

    for step in range(-last, 2):
        if step != 0:
            @pl.when((z + step >= 0) & (z + step <= last))
            def _(step=step):
                line(step).start()
    taps_all[z] = taps_own[...]
    run(PLAN[1])

    loads[3].wait()
    per = BLOCK // GROUP
    for piece in range(groups // per):
        row = skip_v[piece * BLOCK:(piece + 1) * BLOCK].reshape(1, BLOCK)
        skip_rows[piece * per:(piece + 1) * per] = jnp.broadcast_to(row, (BLOCK, BLOCK)).T.reshape(per, GROUP, BLOCK)

    run(PLAN[2])

    @pl.when(z < last - 1)
    def _():
        pl.semaphore_wait(credit, last - 1 - z)

    for step in range(2, planes):
        @pl.when(z + step <= last)
        def _(step=step):
            line(step).start()

    run(PLAN[3])

    u = lax.broadcasted_iota(jnp.int32, (BLOCK, BLOCK), 0)
    t = lax.broadcasted_iota(jnp.int32, (BLOCK, BLOCK), 1)
    reached = t >= u

    def turn(lag, g):
        row = taps_row[lag, pl.ds(g, 1), :]
        return pltpu.roll(jnp.broadcast_to(row, (BLOCK, BLOCK)), 0, 1, stride=1, stride_axis=0)

    def rows_of(lags):
        for lag in lags:
            @pl.when(z != lag)
            def _(lag=lag):
                pltpu.make_async_copy(taps_own, taps_own, line_recv.at[lag]).wait()
            taps_row[lag] = taps_all[lag].astype(f32)

    def build(lags, g):
        before = turn(lags[0] - 1, g) if lags[0] else jnp.zeros((BLOCK, BLOCK), f32)
        for lag in lags:
            turned = turn(lag, g)
            toeplitz[g, lag * BLOCK:(lag + 1) * BLOCK, :] = jnp.where(reached, turned, before).astype(bf16)
            before = turned

    early, late = range(0, LAGS // 2), range(LAGS // 2, LAGS)
    rows_of(early)

    @pl.loop(0, groups, unroll=2)
    def _(g):
        build(early, g)

    rows_of(late)

    back_copies = []
    for chunk in range(CHUNKS):
        rows = pl.ds(chunk * part, part)
        if ("f", chunk) not in sum(PLAN, ()):
            wait_own(chunk)

        @pl.when(z > 0)
        def _(chunk=chunk):
            pltpu.make_async_copy(landed, landed, halo_recv.at[chunk]).wait()

        @pl.loop(chunk * part, (chunk + 1) * part, unroll=part)
        def _(g):
            build(late, g)
            total = jnp.broadcast_to(skip_rows[g][None], (PLANE, GROUP, BLOCK)).reshape(BLOCK, BLOCK)
            total = total * source[g, LAGS - 1:LAGS - 1 + PLANE].reshape(BLOCK, BLOCK).astype(f32)
            windows = [source[g, LAGS - 1 - lag:LAGS - 1 - lag + PLANE].reshape(BLOCK, BLOCK) for lag in range(LAGS)]
            total = total + jnp.dot(jnp.concatenate(windows, axis=1), toeplitz[g], preferred_element_type=f32)
            result[:, g] = total.astype(bf16).reshape(PLANE, GROUP, BLOCK)

        for to in places[:-1]:
            copy = remote(result.at[to, rows], back.at[me, rows], back_send, back_recv, at(z, to))
            copy.start()
            back_copies.append(copy)
    home = pltpu.make_async_copy(result.at[me], back.at[me], local_sem.at[CHUNKS])
    home.start()
    home.wait()

    for copy in tap_copies + own_copies + back_copies:
        copy.wait_send()
    for step in range(1, planes):
        line(1).wait_send()

    @pl.when((z < last) & (me > 0))
    def _():
        for what, chunk in sum(PLAN, ()):
            if what == "h":
                for _ in range(PLANE):
                    halo(me, chunk).wait_send()

    @pl.when(z < last)
    def _():
        for what, chunk in sum(PLAN, ()):
            if what == "f":
                forward(chunk).wait_send()

    pltpu.make_async_copy(back.at[0:PLANE - 1], back.at[0:PLANE - 1], back_recv).wait()


def gate(back_ref, q_ref, out_ref):
    for first in range(0, q_ref.shape[1], BLOCK):
        lanes = slice(first, first + BLOCK)
        turned = back_ref[lanes, :].astype(jnp.float32).T
        out_ref[:, lanes] = (q_ref[:, lanes].astype(jnp.float32) * turned).astype(jnp.bfloat16)


def solution(mesh):
    planes = mesh.shape["ctx"] // PLANE

    def per_device(query, key, value, filter_taps, skip):
        tokens, channels = query.shape
        groups = channels // GROUP // PLANE
        hbm = pl.BlockSpec(memory_space=pl.ANY)
        bf16, f32 = jnp.bfloat16, jnp.float32
        dma = pltpu.SemaphoreType.DMA
        back = pl.pallas_call(
            functools.partial(kernel, planes),
            out_shape=jax.ShapeDtypeStruct((PLANE, groups, GROUP, BLOCK), bf16),
            in_specs=[hbm] * 4,
            out_specs=hbm,
            scratch_shapes=[
                pltpu.VMEM((tokens, channels), bf16),
                pltpu.VMEM((tokens, channels), bf16),
                pltpu.VMEM((groups * GROUP,), f32),
                pltpu.VMEM((groups, GROUP, BLOCK), f32),
                pltpu.VMEM((PLANE, groups, GROUP, BLOCK), bf16),
                pltpu.VMEM((groups, LAGS - 1 + PLANE, GROUP, BLOCK), bf16),
                pltpu.VMEM((PLANE, BLOCK // PLANE, BLOCK), bf16),
                pltpu.VMEM((BLOCK, BLOCK), f32),
                pltpu.VMEM((groups, BLOCK), bf16),
                pltpu.VMEM((planes, groups, BLOCK), bf16),
                pltpu.VMEM((planes, groups, BLOCK), f32),
                pltpu.VMEM((groups, LAGS * BLOCK, BLOCK), bf16),
                pltpu.VMEM((PLANE, groups, GROUP, BLOCK), bf16),
                dma((4,)), dma((CHUNKS + 1,)),
                dma, dma, dma, dma((planes,)),
                pltpu.SemaphoreType.REGULAR,
                dma, dma((CHUNKS,)), dma((2,)), dma((CHUNKS,)), dma, dma,
            ],
            compiler_params=pltpu.CompilerParams(collective_id=0, has_side_effects=True),
        )(key, value, filter_taps, skip)
        steps = STEPS
        return pl.pallas_call(
            gate,
            grid=(steps,),
            out_shape=jax.ShapeDtypeStruct((tokens, channels), bf16),
            in_specs=[pl.BlockSpec((channels // steps, BLOCK), lambda i: (i, 0)), pl.BlockSpec((tokens, channels // steps), lambda i: (0, i))],
            out_specs=pl.BlockSpec((tokens, channels // steps), lambda i: (0, i)),
        )(back.reshape(channels, BLOCK), query)

    placed = (P("ctx", "ch"), P("ctx", "ch"), P("ctx", "ch"), P("ctx", "ch"), P("ch"))
    return jax.shard_map(per_device, mesh=mesh, in_specs=placed, out_specs=P("ctx", "ch"), check_vma=False)
```

```python
import functools

import jax
import jax.numpy as jnp
from jax import lax
from jax.experimental import pallas as pl
from jax.experimental.pallas import tpu as pltpu
from jax.sharding import PartitionSpec as P

MESH = pl.DeviceIdType.MESH
GROUP = 16
BLOCK = 128
LAGS = 8
PLANE = 8
PLAN = ((('m', 0), ('m', 1), ('o', 3), ('o', 0), ('h', 0), ('h', 1)), (('h', 2), ('o', 1), ('o', 2)), (('f', 3),), ())
STEPS = 2
CHUNKS = 4


def kernel(planes, k_hbm, v_hbm, taps_hbm, skip_hbm, back,
           k_v, v_v, skip_v, skip_rows, mixed, source, taps_in, taps_f, taps_own, taps_all, taps_row,
           toeplitz, result,
           load_sem, local_sem, tap_send, tap_recv, line_send, line_recv, credit,
           own_send, own_recv, halo_send, halo_recv, back_send, back_recv):
    ctx, ch = lax.axis_index("ctx"), lax.axis_index("ch")
    z, me = ctx // PLANE, ctx % PLANE
    last = planes - 1
    groups = source.shape[0]
    half = groups // 2
    width = half * GROUP
    part = groups // CHUNKS
    f32, bf16 = jnp.float32, jnp.bfloat16

    def at(plane, place):
        return (plane * PLANE + place, ch)

    def remote(src, dst, send, recv, device):
        return pltpu.make_async_remote_copy(
            src_ref=src, dst_ref=dst, send_sem=send, recv_sem=recv,
            device_id=device, device_id_type=MESH)

    barrier = pltpu.get_barrier_semaphore()
    for step in range(1, PLANE):
        pl.semaphore_signal(barrier, inc=1, device_id=at(z, (me + step) % PLANE), device_id_type=MESH)

    @pl.when(z > 0)
    def _():
        for step in range(PLANE):
            pl.semaphore_signal(barrier, inc=1, device_id=at(z - 1, (me + step) % PLANE), device_id_type=MESH)

    for step in range(1, planes):
        @pl.when(z + step < planes)
        def _(step=step):
            pl.semaphore_signal(barrier, inc=1, device_id=at(z + step, me), device_id_type=MESH)

    loads = [
        pltpu.make_async_copy(k_hbm, k_v, load_sem.at[0]),
        pltpu.make_async_copy(v_hbm, v_v, load_sem.at[1]),
        pltpu.make_async_copy(taps_hbm, taps_in.at[me], load_sem.at[2]),
        pltpu.make_async_copy(skip_hbm.at[pl.ds(pl.multiple_of(me * groups * GROUP, 256), groups * GROUP)], skip_v, load_sem.at[3]),
    ]
    for load in loads:
        load.start()

    @pl.when(z == 0)
    def _():
        source[:, 0:LAGS - 1] = jnp.zeros((groups, LAGS - 1, GROUP, BLOCK), bf16)

    pl.semaphore_wait(barrier, PLANE - 1 + z + jnp.where(z < last, PLANE, 0))

    tap_copies = []
    for step in range(1, PLANE):
        copy = remote(taps_hbm, taps_in.at[me], tap_send, tap_recv, at(z, (me + step) % PLANE))
        copy.start()
        tap_copies.append(copy)

    for step in range(2, planes):
        @pl.when(z - step >= 0)
        def _(step=step):
            pl.semaphore_signal(credit, inc=1, device_id=at(z - step, me), device_id_type=MESH)

    loads[0].wait()
    loads[1].wait()
    own_copies = []
    local_copies = {}
    pieces = [pl.ds(chunk * part, part) for chunk in range(CHUNKS)]

    def mix(to, which):
        lanes = pl.ds(pl.multiple_of(to * groups * GROUP + which * width, width), width)
        m = (k_v[:, lanes].astype(f32) * v_v[:, lanes].astype(f32)).T
        mixed[to, pl.ds(which * half, half)] = m.astype(bf16).reshape(half, GROUP, BLOCK)

    def send_own(chunk):
        for to in places[:-1]:
            copy = remote(mixed.at[to, pieces[chunk]], source.at[pieces[chunk], LAGS - 1 + me], own_send, own_recv.at[chunk], at(z, to))
            copy.start()
            own_copies.append(copy)
        copy = pltpu.make_async_copy(mixed.at[me, pieces[chunk]], source.at[pieces[chunk], LAGS - 1 + me], local_sem.at[chunk])
        copy.start()
        local_copies[chunk] = copy

    def halo(to, chunk):
        return remote(mixed.at[to, pieces[chunk]], source.at[pieces[chunk], jnp.maximum(me - 1, 0)], halo_send.at[0], halo_recv.at[chunk],
                      at(jnp.minimum(z + 1, last), to))

    def send_halo(chunk):
        @pl.when((z < last) & (me > 0))
        def _():
            for to in places:
                halo(to, chunk).start()

    def forward(chunk):
        return remote(source.at[pieces[chunk], LAGS:LAGS + PLANE - 1], source.at[pieces[chunk], 0:LAGS - 1], halo_send.at[1],
                      halo_recv.at[chunk], at(jnp.minimum(z + 1, last), me))

    landed = mixed.at[0:PLANE - 1, pl.ds(0, part)]

    def wait_own(chunk):
        local_copies[chunk].wait()
        pltpu.make_async_copy(landed, landed, own_recv.at[chunk]).wait()

    def send_forward(chunk):
        wait_own(chunk)

        @pl.when(z < last)
        def _():
            forward(chunk).start()

    places = [(me + step) % PLANE for step in range(1, PLANE)] + [me]

    def run(stage):
        for what, which in stage:
            if what == "m":
                for to in places:
                    mix(to, which)
            if what == "o":
                send_own(which)
            if what == "h":
                send_halo(which)
            if what == "f":
                send_forward(which)

    run(PLAN[0])

    loads[2].wait()
    pltpu.make_async_copy(taps_in.at[0:PLANE - 1], taps_in.at[0:PLANE - 1], tap_recv).wait()
    taps_f[...] = taps_in[...].astype(f32).reshape(BLOCK, BLOCK).T
    taps_own[...] = taps_f[pl.ds(pl.multiple_of(me * groups, groups), groups), :].astype(bf16)

    def line(step):
        return remote(taps_own, taps_all.at[z], line_send, line_recv.at[z], at(jnp.clip(z + step, 0, last), me))

    for step in range(-last, 2):
        if step != 0:
            @pl.when((z + step >= 0) & (z + step <= last))
            def _(step=step):
                line(step).start()
    taps_all[z] = taps_own[...]
    run(PLAN[1])

    @pl.when(z < last - 1)
    def _():
        pl.semaphore_wait(credit, last - 1 - z)

    for step in range(2, planes):
        @pl.when(z + step <= last)
        def _(step=step):
            line(step).start()

    loads[3].wait()
    per = BLOCK // GROUP
    for piece in range(groups // per):
        row = skip_v[piece * BLOCK:(piece + 1) * BLOCK].reshape(1, BLOCK)
        skip_rows[piece * per:(piece + 1) * per] = jnp.broadcast_to(row, (BLOCK, BLOCK)).T.reshape(per, GROUP, BLOCK)

    run(PLAN[2])


    run(PLAN[3])

    u = lax.broadcasted_iota(jnp.int32, (BLOCK, BLOCK), 0)
    t = lax.broadcasted_iota(jnp.int32, (BLOCK, BLOCK), 1)
    reached = t >= u

    def turn(lag, g):
        row = taps_row[lag, pl.ds(g, 1), :]
        return pltpu.roll(jnp.broadcast_to(row, (BLOCK, BLOCK)), 0, 1, stride=1, stride_axis=0)

    def rows_of(lags):
        for lag in lags:
            @pl.when(z != lag)
            def _(lag=lag):
                pltpu.make_async_copy(taps_own, taps_own, line_recv.at[lag]).wait()
            taps_row[lag] = taps_all[lag].astype(f32)

    def build(lags, g):
        before = turn(lags[0] - 1, g) if lags[0] else jnp.zeros((BLOCK, BLOCK), f32)
        for lag in lags:
            turned = turn(lag, g)
            toeplitz[g, lag * BLOCK:(lag + 1) * BLOCK, :] = jnp.where(reached, turned, before).astype(bf16)
            before = turned

    early, late = range(0, LAGS // 2), range(LAGS // 2, LAGS)
    rows_of(early)

    @pl.loop(0, groups, unroll=2)
    def _(g):
        build(early, g)

    rows_of(late)

    back_copies = []
    for chunk in range(CHUNKS):
        rows = pl.ds(chunk * part, part)
        if ("f", chunk) not in sum(PLAN, ()):
            wait_own(chunk)

        @pl.when(z > 0)
        def _(chunk=chunk):
            pltpu.make_async_copy(landed, landed, halo_recv.at[chunk]).wait()

        @pl.loop(chunk * part, (chunk + 1) * part, unroll=part)
        def _(g):
            build(late, g)
            total = jnp.broadcast_to(skip_rows[g][None], (PLANE, GROUP, BLOCK)).reshape(BLOCK, BLOCK)
            total = total * source[g, LAGS - 1:LAGS - 1 + PLANE].reshape(BLOCK, BLOCK).astype(f32)
            windows = [source[g, LAGS - 1 - lag:LAGS - 1 - lag + PLANE].reshape(BLOCK, BLOCK) for lag in range(LAGS)]
            total = total + jnp.dot(jnp.concatenate(windows, axis=1), toeplitz[g], preferred_element_type=f32)
            result[:, g] = total.astype(bf16).reshape(PLANE, GROUP, BLOCK)

        for to in places[:-1]:
            copy = remote(result.at[to, rows], back.at[me, rows], back_send, back_recv, at(z, to))
            copy.start()
            back_copies.append(copy)
    home = pltpu.make_async_copy(result.at[me], back.at[me], local_sem.at[CHUNKS])
    home.start()
    home.wait()

    for copy in tap_copies + own_copies + back_copies:
        copy.wait_send()
    for step in range(1, planes):
        line(1).wait_send()

    @pl.when((z < last) & (me > 0))
    def _():
        for what, chunk in sum(PLAN, ()):
            if what == "h":
                for _ in range(PLANE):
                    halo(me, chunk).wait_send()

    @pl.when(z < last)
    def _():
        for what, chunk in sum(PLAN, ()):
            if what == "f":
                forward(chunk).wait_send()

    pltpu.make_async_copy(back.at[0:PLANE - 1], back.at[0:PLANE - 1], back_recv).wait()


def gate(back_ref, q_ref, out_ref):
    for first in range(0, q_ref.shape[1], BLOCK):
        lanes = slice(first, first + BLOCK)
        turned = back_ref[lanes, :].astype(jnp.float32).T
        out_ref[:, lanes] = (q_ref[:, lanes].astype(jnp.float32) * turned).astype(jnp.bfloat16)


def solution(mesh):
    planes = mesh.shape["ctx"] // PLANE

    def per_device(query, key, value, filter_taps, skip):
        tokens, channels = query.shape
        groups = channels // GROUP // PLANE
        hbm = pl.BlockSpec(memory_space=pl.ANY)
        bf16, f32 = jnp.bfloat16, jnp.float32
        dma = pltpu.SemaphoreType.DMA
        back = pl.pallas_call(
            functools.partial(kernel, planes),
            out_shape=jax.ShapeDtypeStruct((PLANE, groups, GROUP, BLOCK), bf16),
            in_specs=[hbm] * 4,
            out_specs=hbm,
            scratch_shapes=[
                pltpu.VMEM((tokens, channels), bf16),
                pltpu.VMEM((tokens, channels), bf16),
                pltpu.VMEM((groups * GROUP,), f32),
                pltpu.VMEM((groups, GROUP, BLOCK), f32),
                pltpu.VMEM((PLANE, groups, GROUP, BLOCK), bf16),
                pltpu.VMEM((groups, LAGS - 1 + PLANE, GROUP, BLOCK), bf16),
                pltpu.VMEM((PLANE, BLOCK // PLANE, BLOCK), bf16),
                pltpu.VMEM((BLOCK, BLOCK), f32),
                pltpu.VMEM((groups, BLOCK), bf16),
                pltpu.VMEM((planes, groups, BLOCK), bf16),
                pltpu.VMEM((planes, groups, BLOCK), f32),
                pltpu.VMEM((groups, LAGS * BLOCK, BLOCK), bf16),
                pltpu.VMEM((PLANE, groups, GROUP, BLOCK), bf16),
                dma((4,)), dma((CHUNKS + 1,)),
                dma, dma, dma, dma((planes,)),
                pltpu.SemaphoreType.REGULAR,
                dma, dma((CHUNKS,)), dma((2,)), dma((CHUNKS,)), dma, dma,
            ],
            compiler_params=pltpu.CompilerParams(collective_id=0, has_side_effects=True),
        )(key, value, filter_taps, skip)
        steps = STEPS
        return pl.pallas_call(
            gate,
            grid=(steps,),
            out_shape=jax.ShapeDtypeStruct((tokens, channels), bf16),
            in_specs=[pl.BlockSpec((channels // steps, BLOCK), lambda i: (i, 0)), pl.BlockSpec((tokens, channels // steps), lambda i: (0, i))],
            out_specs=pl.BlockSpec((tokens, channels // steps), lambda i: (0, i)),
        )(back.reshape(channels, BLOCK), query)

    placed = (P("ctx", "ch"), P("ctx", "ch"), P("ctx", "ch"), P("ctx", "ch"), P("ch"))
    return jax.shard_map(per_device, mesh=mesh, in_specs=placed, out_specs=P("ctx", "ch"), check_vma=False)
```

```python
import functools

import jax
import jax.numpy as jnp
from jax import lax
from jax.experimental import pallas as pl
from jax.experimental.pallas import tpu as pltpu
from jax.sharding import PartitionSpec as P

MESH = pl.DeviceIdType.MESH
GROUP = 16
BLOCK = 128
LAGS = 8
PLANE = 8
PLAN = ((('m', 0), ('m', 1), ('o', 2), ('h', 0), ('o', 3), ('x', 1)), (('y', 1), ('o', 0), ('o', 1)), (('f', 2), ('f', 3)), ())
STEPS = 2
CHUNKS = 4


def kernel(planes, k_hbm, v_hbm, taps_hbm, skip_hbm, back,
           k_v, v_v, skip_v, skip_rows, mixed, source, taps_in, taps_f, taps_own, taps_all, taps_row,
           toeplitz, result,
           load_sem, local_sem, tap_send, tap_recv, line_send, line_recv, credit,
           own_send, own_recv, halo_send, halo_recv, back_send, back_recv):
    ctx, ch = lax.axis_index("ctx"), lax.axis_index("ch")
    z, me = ctx // PLANE, ctx % PLANE
    last = planes - 1
    groups = source.shape[0]
    half = groups // 2
    width = half * GROUP
    part = groups // CHUNKS
    f32, bf16 = jnp.float32, jnp.bfloat16

    def at(plane, place):
        return (plane * PLANE + place, ch)

    def remote(src, dst, send, recv, device):
        return pltpu.make_async_remote_copy(
            src_ref=src, dst_ref=dst, send_sem=send, recv_sem=recv,
            device_id=device, device_id_type=MESH)

    barrier = pltpu.get_barrier_semaphore()
    for step in range(1, PLANE):
        pl.semaphore_signal(barrier, inc=1, device_id=at(z, (me + step) % PLANE), device_id_type=MESH)

    @pl.when(z > 0)
    def _():
        for step in range(PLANE):
            pl.semaphore_signal(barrier, inc=1, device_id=at(z - 1, (me + step) % PLANE), device_id_type=MESH)

    for step in range(1, planes):
        @pl.when(z + step < planes)
        def _(step=step):
            pl.semaphore_signal(barrier, inc=1, device_id=at(z + step, me), device_id_type=MESH)

    loads = [
        pltpu.make_async_copy(k_hbm, k_v, load_sem.at[0]),
        pltpu.make_async_copy(v_hbm, v_v, load_sem.at[1]),
        pltpu.make_async_copy(taps_hbm, taps_in.at[me], load_sem.at[2]),
        pltpu.make_async_copy(skip_hbm.at[pl.ds(pl.multiple_of(me * groups * GROUP, 256), groups * GROUP)], skip_v, load_sem.at[3]),
    ]
    for load in loads:
        load.start()

    @pl.when(z == 0)
    def _():
        source[:, 0:LAGS - 1] = jnp.zeros((groups, LAGS - 1, GROUP, BLOCK), bf16)

    pl.semaphore_wait(barrier, PLANE - 1 + z + jnp.where(z < last, PLANE, 0))

    tap_copies = []
    for step in range(1, PLANE):
        copy = remote(taps_hbm, taps_in.at[me], tap_send, tap_recv, at(z, (me + step) % PLANE))
        copy.start()
        tap_copies.append(copy)

    for step in range(2, planes):
        @pl.when(z - step >= 0)
        def _(step=step):
            pl.semaphore_signal(credit, inc=1, device_id=at(z - step, me), device_id_type=MESH)

    loads[0].wait()
    loads[1].wait()
    own_copies = []
    local_copies = {}
    pieces = [pl.ds(chunk * part, part) for chunk in range(CHUNKS)]

    def mix(to, which):
        lanes = pl.ds(pl.multiple_of(to * groups * GROUP + which * width, width), width)
        m = (k_v[:, lanes].astype(f32) * v_v[:, lanes].astype(f32)).T
        mixed[to, pl.ds(which * half, half)] = m.astype(bf16).reshape(half, GROUP, BLOCK)

    def send_own(chunk):
        for to in places[:-1]:
            copy = remote(mixed.at[to, pieces[chunk]], source.at[pieces[chunk], LAGS - 1 + me], own_send, own_recv.at[chunk], at(z, to))
            copy.start()
            own_copies.append(copy)
        copy = pltpu.make_async_copy(mixed.at[me, pieces[chunk]], source.at[pieces[chunk], LAGS - 1 + me], local_sem.at[chunk])
        copy.start()
        local_copies[chunk] = copy

    def halo(to, chunk):
        return remote(mixed.at[to, pieces[chunk]], source.at[pieces[chunk], jnp.maximum(me - 1, 0)], halo_send.at[0], halo_recv.at[chunk],
                      at(jnp.minimum(z + 1, last), to))

    def send_halo(chunk):
        @pl.when((z < last) & (me > 0))
        def _():
            for to in places:
                halo(to, chunk).start()

    def forward(chunk):
        return remote(source.at[pieces[chunk], LAGS:LAGS + PLANE - 1], source.at[pieces[chunk], 0:LAGS - 1], halo_send.at[1],
                      halo_recv.at[chunk], at(jnp.minimum(z + 1, last), me))

    landed = mixed.at[0:PLANE - 1, pl.ds(0, part)]

    def wait_own(chunk):
        local_copies[chunk].wait()
        pltpu.make_async_copy(landed, landed, own_recv.at[chunk]).wait()

    def send_forward(chunk):
        wait_own(chunk)

        @pl.when(z < last)
        def _():
            forward(chunk).start()

    places = [(me + step) % PLANE for step in range(1, PLANE)] + [me]

    def run(stage):
        for what, which in stage:
            if what == "m":
                for to in places:
                    mix(to, which)
            if what == "o":
                send_own(which)
            if what == "h":
                send_halo(which)
            if what == "f":
                send_forward(which)
            if what in "xy":
                @pl.when(ch % 2 == (0 if what == "x" else 1))
                def _(which=which):
                    send_halo(which)

    run(PLAN[0])

    loads[2].wait()
    pltpu.make_async_copy(taps_in.at[0:PLANE - 1], taps_in.at[0:PLANE - 1], tap_recv).wait()
    taps_f[...] = taps_in[...].astype(f32).reshape(BLOCK, BLOCK).T
    taps_own[...] = taps_f[pl.ds(pl.multiple_of(me * groups, groups), groups), :].astype(bf16)

    def line(step):
        return remote(taps_own, taps_all.at[z], line_send, line_recv.at[z], at(jnp.clip(z + step, 0, last), me))

    for step in range(-last, 2):
        if step != 0:
            @pl.when((z + step >= 0) & (z + step <= last))
            def _(step=step):
                line(step).start()
    taps_all[z] = taps_own[...]
    run(PLAN[1])

    @pl.when(z < last - 1)
    def _():
        pl.semaphore_wait(credit, last - 1 - z)

    for step in range(2, planes):
        @pl.when(z + step <= last)
        def _(step=step):
            line(step).start()

    loads[3].wait()
    per = BLOCK // GROUP
    for piece in range(groups // per):
        row = skip_v[piece * BLOCK:(piece + 1) * BLOCK].reshape(1, BLOCK)
        skip_rows[piece * per:(piece + 1) * per] = jnp.broadcast_to(row, (BLOCK, BLOCK)).T.reshape(per, GROUP, BLOCK)

    run(PLAN[2])


    run(PLAN[3])

    u = lax.broadcasted_iota(jnp.int32, (BLOCK, BLOCK), 0)
    t = lax.broadcasted_iota(jnp.int32, (BLOCK, BLOCK), 1)
    reached = t >= u

    def turn(lag, g):
        row = taps_row[lag, pl.ds(g, 1), :]
        return pltpu.roll(jnp.broadcast_to(row, (BLOCK, BLOCK)), 0, 1, stride=1, stride_axis=0)

    def rows_of(lags):
        for lag in lags:
            @pl.when(z != lag)
            def _(lag=lag):
                pltpu.make_async_copy(taps_own, taps_own, line_recv.at[lag]).wait()
            taps_row[lag] = taps_all[lag].astype(f32)

    def build(lags, g):
        before = turn(lags[0] - 1, g) if lags[0] else jnp.zeros((BLOCK, BLOCK), f32)
        for lag in lags:
            turned = turn(lag, g)
            toeplitz[g, lag * BLOCK:(lag + 1) * BLOCK, :] = jnp.where(reached, turned, before).astype(bf16)
            before = turned

    early, late = range(0, LAGS // 2), range(LAGS // 2, LAGS)
    rows_of(early)

    @pl.loop(0, groups, unroll=2)
    def _(g):
        build(early, g)

    rows_of(late)

    back_copies = []
    for chunk in range(CHUNKS):
        rows = pl.ds(chunk * part, part)
        if ("f", chunk) not in sum(PLAN, ()):
            wait_own(chunk)

        @pl.when(z > 0)
        def _(chunk=chunk):
            pltpu.make_async_copy(landed, landed, halo_recv.at[chunk]).wait()

        @pl.loop(chunk * part, (chunk + 1) * part, unroll=part)
        def _(g):
            build(late, g)
            total = jnp.broadcast_to(skip_rows[g][None], (PLANE, GROUP, BLOCK)).reshape(BLOCK, BLOCK)
            total = total * source[g, LAGS - 1:LAGS - 1 + PLANE].reshape(BLOCK, BLOCK).astype(f32)
            windows = [source[g, LAGS - 1 - lag:LAGS - 1 - lag + PLANE].reshape(BLOCK, BLOCK) for lag in range(LAGS)]
            total = total + jnp.dot(jnp.concatenate(windows, axis=1), toeplitz[g], preferred_element_type=f32)
            result[:, g] = total.astype(bf16).reshape(PLANE, GROUP, BLOCK)

        for to in places[:-1]:
            copy = remote(result.at[to, rows], back.at[me, rows], back_send, back_recv, at(z, to))
            copy.start()
            back_copies.append(copy)
    home = pltpu.make_async_copy(result.at[me], back.at[me], local_sem.at[CHUNKS])
    home.start()
    home.wait()

    for copy in tap_copies + own_copies + back_copies:
        copy.wait_send()
    for step in range(1, planes):
        line(1).wait_send()

    @pl.when((z < last) & (me > 0))
    def _():
        for what, chunk in sum(PLAN, ()):
            if what in "hx":
                for _ in range(PLANE):
                    halo(me, chunk).wait_send()

    @pl.when(z < last)
    def _():
        for what, chunk in sum(PLAN, ()):
            if what == "f":
                forward(chunk).wait_send()

    pltpu.make_async_copy(back.at[0:PLANE - 1], back.at[0:PLANE - 1], back_recv).wait()


def gate(back_ref, q_ref, out_ref):
    for first in range(0, q_ref.shape[1], BLOCK):
        lanes = slice(first, first + BLOCK)
        turned = back_ref[lanes, :].astype(jnp.float32).T
        out_ref[:, lanes] = (q_ref[:, lanes].astype(jnp.float32) * turned).astype(jnp.bfloat16)


def solution(mesh):
    planes = mesh.shape["ctx"] // PLANE

    def per_device(query, key, value, filter_taps, skip):
        tokens, channels = query.shape
        groups = channels // GROUP // PLANE
        hbm = pl.BlockSpec(memory_space=pl.ANY)
        bf16, f32 = jnp.bfloat16, jnp.float32
        dma = pltpu.SemaphoreType.DMA
        back = pl.pallas_call(
            functools.partial(kernel, planes),
            out_shape=jax.ShapeDtypeStruct((PLANE, groups, GROUP, BLOCK), bf16),
            in_specs=[hbm] * 4,
            out_specs=hbm,
            scratch_shapes=[
                pltpu.VMEM((tokens, channels), bf16),
                pltpu.VMEM((tokens, channels), bf16),
                pltpu.VMEM((groups * GROUP,), f32),
                pltpu.VMEM((groups, GROUP, BLOCK), f32),
                pltpu.VMEM((PLANE, groups, GROUP, BLOCK), bf16),
                pltpu.VMEM((groups, LAGS - 1 + PLANE, GROUP, BLOCK), bf16),
                pltpu.VMEM((PLANE, BLOCK // PLANE, BLOCK), bf16),
                pltpu.VMEM((BLOCK, BLOCK), f32),
                pltpu.VMEM((groups, BLOCK), bf16),
                pltpu.VMEM((planes, groups, BLOCK), bf16),
                pltpu.VMEM((planes, groups, BLOCK), f32),
                pltpu.VMEM((groups, LAGS * BLOCK, BLOCK), bf16),
                pltpu.VMEM((PLANE, groups, GROUP, BLOCK), bf16),
                dma((4,)), dma((CHUNKS + 1,)),
                dma, dma, dma, dma((planes,)),
                pltpu.SemaphoreType.REGULAR,
                dma, dma((CHUNKS,)), dma((2,)), dma((CHUNKS,)), dma, dma,
            ],
            compiler_params=pltpu.CompilerParams(collective_id=0, has_side_effects=True),
        )(key, value, filter_taps, skip)
        steps = STEPS
        return pl.pallas_call(
            gate,
            grid=(steps,),
            out_shape=jax.ShapeDtypeStruct((tokens, channels), bf16),
            in_specs=[pl.BlockSpec((channels // steps, BLOCK), lambda i: (i, 0)), pl.BlockSpec((tokens, channels // steps), lambda i: (0, i))],
            out_specs=pl.BlockSpec((tokens, channels // steps), lambda i: (0, i)),
        )(back.reshape(channels, BLOCK), query)

    placed = (P("ctx", "ch"), P("ctx", "ch"), P("ctx", "ch"), P("ctx", "ch"), P("ch"))
    return jax.shard_map(per_device, mesh=mesh, in_specs=placed, out_specs=P("ctx", "ch"), check_vma=False)
```

```python
import functools

import jax
import jax.numpy as jnp
from jax import lax
from jax.experimental import pallas as pl
from jax.experimental.pallas import tpu as pltpu
from jax.sharding import PartitionSpec as P

MESH = pl.DeviceIdType.MESH
GROUP = 16
BLOCK = 128
LAGS = 8
PLANE = 8
PLAN = ((('m', 0), ('m', 1), ('o', 2), ('h', 0), ('o', 3), ('x', 1)), (('o', 0), ('y', 1), ('o', 1)), (('f', 2), ('f', 3)), ())
STEPS = 2
CHUNKS = 4


def kernel(planes, k_hbm, v_hbm, taps_hbm, skip_hbm, back,
           k_v, v_v, skip_v, skip_rows, mixed, source, taps_in, taps_f, taps_own, taps_all, taps_row,
           toeplitz, result,
           load_sem, local_sem, tap_send, tap_recv, line_send, line_recv, credit,
           own_send, own_recv, halo_send, halo_recv, back_send, back_recv):
    ctx, ch = lax.axis_index("ctx"), lax.axis_index("ch")
    z, me = ctx // PLANE, ctx % PLANE
    last = planes - 1
    groups = source.shape[0]
    half = groups // 2
    width = half * GROUP
    part = groups // CHUNKS
    f32, bf16 = jnp.float32, jnp.bfloat16

    def at(plane, place):
        return (plane * PLANE + place, ch)

    def remote(src, dst, send, recv, device):
        return pltpu.make_async_remote_copy(
            src_ref=src, dst_ref=dst, send_sem=send, recv_sem=recv,
            device_id=device, device_id_type=MESH)

    barrier = pltpu.get_barrier_semaphore()
    for step in range(1, PLANE):
        pl.semaphore_signal(barrier, inc=1, device_id=at(z, (me + step) % PLANE), device_id_type=MESH)

    @pl.when(z > 0)
    def _():
        for step in range(PLANE):
            pl.semaphore_signal(barrier, inc=1, device_id=at(z - 1, (me + step) % PLANE), device_id_type=MESH)

    for step in range(1, planes):
        @pl.when(z + step < planes)
        def _(step=step):
            pl.semaphore_signal(barrier, inc=1, device_id=at(z + step, me), device_id_type=MESH)

    loads = [
        pltpu.make_async_copy(k_hbm, k_v, load_sem.at[0]),
        pltpu.make_async_copy(v_hbm, v_v, load_sem.at[1]),
        pltpu.make_async_copy(taps_hbm, taps_in.at[me], load_sem.at[2]),
        pltpu.make_async_copy(skip_hbm.at[pl.ds(pl.multiple_of(me * groups * GROUP, 256), groups * GROUP)], skip_v, load_sem.at[3]),
    ]
    for load in loads:
        load.start()

    @pl.when(z == 0)
    def _():
        source[:, 0:LAGS - 1] = jnp.zeros((groups, LAGS - 1, GROUP, BLOCK), bf16)

    pl.semaphore_wait(barrier, PLANE - 1 + z + jnp.where(z < last, PLANE, 0))

    tap_copies = []
    for step in range(1, PLANE):
        copy = remote(taps_hbm, taps_in.at[me], tap_send, tap_recv, at(z, (me + step) % PLANE))
        copy.start()
        tap_copies.append(copy)

    for step in range(2, planes):
        @pl.when(z - step >= 0)
        def _(step=step):
            pl.semaphore_signal(credit, inc=1, device_id=at(z - step, me), device_id_type=MESH)

    loads[0].wait()
    loads[1].wait()
    own_copies = []
    local_copies = {}
    pieces = [pl.ds(chunk * part, part) for chunk in range(CHUNKS)]

    def mix(to, which):
        lanes = pl.ds(pl.multiple_of(to * groups * GROUP + which * width, width), width)
        m = (k_v[:, lanes].astype(f32) * v_v[:, lanes].astype(f32)).T
        mixed[to, pl.ds(which * half, half)] = m.astype(bf16).reshape(half, GROUP, BLOCK)

    def send_own(chunk):
        for to in places[:-1]:
            copy = remote(mixed.at[to, pieces[chunk]], source.at[pieces[chunk], LAGS - 1 + me], own_send, own_recv.at[chunk], at(z, to))
            copy.start()
            own_copies.append(copy)
        copy = pltpu.make_async_copy(mixed.at[me, pieces[chunk]], source.at[pieces[chunk], LAGS - 1 + me], local_sem.at[chunk])
        copy.start()
        local_copies[chunk] = copy

    def halo(to, chunk):
        return remote(mixed.at[to, pieces[chunk]], source.at[pieces[chunk], jnp.maximum(me - 1, 0)], halo_send.at[0], halo_recv.at[chunk],
                      at(jnp.minimum(z + 1, last), to))

    def send_halo(chunk):
        @pl.when((z < last) & (me > 0))
        def _():
            for to in places:
                halo(to, chunk).start()

    def forward(chunk):
        return remote(source.at[pieces[chunk], LAGS:LAGS + PLANE - 1], source.at[pieces[chunk], 0:LAGS - 1], halo_send.at[1],
                      halo_recv.at[chunk], at(jnp.minimum(z + 1, last), me))

    landed = mixed.at[0:PLANE - 1, pl.ds(0, part)]

    def wait_own(chunk):
        local_copies[chunk].wait()
        pltpu.make_async_copy(landed, landed, own_recv.at[chunk]).wait()

    def send_forward(chunk):
        wait_own(chunk)

        @pl.when(z < last)
        def _():
            forward(chunk).start()

    places = [(me + step) % PLANE for step in range(1, PLANE)] + [me]

    def run(stage):
        for what, which in stage:
            if what == "m":
                for to in places:
                    mix(to, which)
            if what == "o":
                send_own(which)
            if what == "h":
                send_halo(which)
            if what == "f":
                send_forward(which)
            if what in "xy":
                @pl.when(ch % 2 == (0 if what == "x" else 1))
                def _(which=which):
                    send_halo(which)

    run(PLAN[0])

    loads[2].wait()
    pltpu.make_async_copy(taps_in.at[0:PLANE - 1], taps_in.at[0:PLANE - 1], tap_recv).wait()
    taps_f[...] = taps_in[...].astype(f32).reshape(BLOCK, BLOCK).T
    taps_own[...] = taps_f[pl.ds(pl.multiple_of(me * groups, groups), groups), :].astype(bf16)

    def line(step):
        return remote(taps_own, taps_all.at[z], line_send, line_recv.at[z], at(jnp.clip(z + step, 0, last), me))

    for step in range(-last, 2):
        if step != 0:
            @pl.when((z + step >= 0) & (z + step <= last))
            def _(step=step):
                line(step).start()
    taps_all[z] = taps_own[...]
    run(PLAN[1])

    @pl.when(z < last - 1)
    def _():
        pl.semaphore_wait(credit, last - 1 - z)

    for step in range(2, planes):
        @pl.when(z + step <= last)
        def _(step=step):
            line(step).start()

    loads[3].wait()
    per = BLOCK // GROUP
    for piece in range(groups // per):
        row = skip_v[piece * BLOCK:(piece + 1) * BLOCK].reshape(1, BLOCK)
        skip_rows[piece * per:(piece + 1) * per] = jnp.broadcast_to(row, (BLOCK, BLOCK)).T.reshape(per, GROUP, BLOCK)

    run(PLAN[2])


    run(PLAN[3])

    u = lax.broadcasted_iota(jnp.int32, (BLOCK, BLOCK), 0)
    t = lax.broadcasted_iota(jnp.int32, (BLOCK, BLOCK), 1)
    reached = t >= u

    def turn(lag, g):
        row = taps_row[lag, pl.ds(g, 1), :]
        return pltpu.roll(jnp.broadcast_to(row, (BLOCK, BLOCK)), 0, 1, stride=1, stride_axis=0)

    def rows_of(lags):
        for lag in lags:
            @pl.when(z != lag)
            def _(lag=lag):
                pltpu.make_async_copy(taps_own, taps_own, line_recv.at[lag]).wait()
            taps_row[lag] = taps_all[lag].astype(f32)

    def build(lags, g):
        before = turn(lags[0] - 1, g) if lags[0] else jnp.zeros((BLOCK, BLOCK), f32)
        for lag in lags:
            turned = turn(lag, g)
            toeplitz[g, lag * BLOCK:(lag + 1) * BLOCK, :] = jnp.where(reached, turned, before).astype(bf16)
            before = turned

    early, late = range(0, LAGS // 2), range(LAGS // 2, LAGS)
    rows_of(early)

    @pl.loop(0, groups, unroll=2)
    def _(g):
        build(early, g)

    rows_of(late)

    back_copies = []
    for chunk in range(CHUNKS):
        rows = pl.ds(chunk * part, part)
        if ("f", chunk) not in sum(PLAN, ()):
            wait_own(chunk)

        @pl.when(z > 0)
        def _(chunk=chunk):
            pltpu.make_async_copy(landed, landed, halo_recv.at[chunk]).wait()

        @pl.loop(chunk * part, (chunk + 1) * part, unroll=part)
        def _(g):
            build(late, g)
            total = jnp.broadcast_to(skip_rows[g][None], (PLANE, GROUP, BLOCK)).reshape(BLOCK, BLOCK)
            total = total * source[g, LAGS - 1:LAGS - 1 + PLANE].reshape(BLOCK, BLOCK).astype(f32)
            windows = [source[g, LAGS - 1 - lag:LAGS - 1 - lag + PLANE].reshape(BLOCK, BLOCK) for lag in range(LAGS)]
            total = total + jnp.dot(jnp.concatenate(windows, axis=1), toeplitz[g], preferred_element_type=f32)
            result[:, g] = total.astype(bf16).reshape(PLANE, GROUP, BLOCK)

        for to in places[:-1]:
            copy = remote(result.at[to, rows], back.at[me, rows], back_send, back_recv, at(z, to))
            copy.start()
            back_copies.append(copy)
    home = pltpu.make_async_copy(result.at[me], back.at[me], local_sem.at[CHUNKS])
    home.start()
    home.wait()

    for copy in tap_copies + own_copies + back_copies:
        copy.wait_send()
    for step in range(1, planes):
        line(1).wait_send()

    @pl.when((z < last) & (me > 0))
    def _():
        for what, chunk in sum(PLAN, ()):
            if what in "hx":
                for _ in range(PLANE):
                    halo(me, chunk).wait_send()

    @pl.when(z < last)
    def _():
        for what, chunk in sum(PLAN, ()):
            if what == "f":
                forward(chunk).wait_send()

    pltpu.make_async_copy(back.at[0:PLANE - 1], back.at[0:PLANE - 1], back_recv).wait()


def gate(back_ref, q_ref, out_ref):
    for first in range(0, q_ref.shape[1], BLOCK):
        lanes = slice(first, first + BLOCK)
        turned = back_ref[lanes, :].astype(jnp.float32).T
        out_ref[:, lanes] = (q_ref[:, lanes].astype(jnp.float32) * turned).astype(jnp.bfloat16)


def solution(mesh):
    planes = mesh.shape["ctx"] // PLANE

    def per_device(query, key, value, filter_taps, skip):
        tokens, channels = query.shape
        groups = channels // GROUP // PLANE
        hbm = pl.BlockSpec(memory_space=pl.ANY)
        bf16, f32 = jnp.bfloat16, jnp.float32
        dma = pltpu.SemaphoreType.DMA
        back = pl.pallas_call(
            functools.partial(kernel, planes),
            out_shape=jax.ShapeDtypeStruct((PLANE, groups, GROUP, BLOCK), bf16),
            in_specs=[hbm] * 4,
            out_specs=hbm,
            scratch_shapes=[
                pltpu.VMEM((tokens, channels), bf16),
                pltpu.VMEM((tokens, channels), bf16),
                pltpu.VMEM((groups * GROUP,), f32),
                pltpu.VMEM((groups, GROUP, BLOCK), f32),
                pltpu.VMEM((PLANE, groups, GROUP, BLOCK), bf16),
                pltpu.VMEM((groups, LAGS - 1 + PLANE, GROUP, BLOCK), bf16),
                pltpu.VMEM((PLANE, BLOCK // PLANE, BLOCK), bf16),
                pltpu.VMEM((BLOCK, BLOCK), f32),
                pltpu.VMEM((groups, BLOCK), bf16),
                pltpu.VMEM((planes, groups, BLOCK), bf16),
                pltpu.VMEM((planes, groups, BLOCK), f32),
                pltpu.VMEM((groups, LAGS * BLOCK, BLOCK), bf16),
                pltpu.VMEM((PLANE, groups, GROUP, BLOCK), bf16),
                dma((4,)), dma((CHUNKS + 1,)),
                dma, dma, dma, dma((planes,)),
                pltpu.SemaphoreType.REGULAR,
                dma, dma((CHUNKS,)), dma((2,)), dma((CHUNKS,)), dma, dma,
            ],
            compiler_params=pltpu.CompilerParams(collective_id=0, has_side_effects=True),
        )(key, value, filter_taps, skip)
        steps = STEPS
        return pl.pallas_call(
            gate,
            grid=(steps,),
            out_shape=jax.ShapeDtypeStruct((tokens, channels), bf16),
            in_specs=[pl.BlockSpec((channels // steps, BLOCK), lambda i: (i, 0)), pl.BlockSpec((tokens, channels // steps), lambda i: (0, i))],
            out_specs=pl.BlockSpec((tokens, channels // steps), lambda i: (0, i)),
        )(back.reshape(channels, BLOCK), query)

    placed = (P("ctx", "ch"), P("ctx", "ch"), P("ctx", "ch"), P("ctx", "ch"), P("ch"))
    return jax.shard_map(per_device, mesh=mesh, in_specs=placed, out_specs=P("ctx", "ch"), check_vma=False)
```

```python
import functools

import jax
import jax.numpy as jnp
from jax import lax
from jax.experimental import pallas as pl
from jax.experimental.pallas import tpu as pltpu
from jax.sharding import PartitionSpec as P

MESH = pl.DeviceIdType.MESH
GROUP = 16
BLOCK = 128
LAGS = 8
PLANE = 8
PLAN = ((('m', 1), ('o', 2), ('m', 0), ('h', 0), ('o', 3), ('x', 1)), (('o', 0), ('y', 1), ('o', 1)), (('f', 2), ('f', 3)), ())
STEPS = 2
CHUNKS = 4


def kernel(planes, k_hbm, v_hbm, taps_hbm, skip_hbm, back,
           k_v, v_v, skip_v, skip_rows, mixed, source, taps_in, taps_f, taps_own, taps_all, taps_row,
           toeplitz, result,
           load_sem, local_sem, tap_send, tap_recv, line_send, line_recv, credit,
           own_send, own_recv, halo_send, halo_recv, back_send, back_recv):
    ctx, ch = lax.axis_index("ctx"), lax.axis_index("ch")
    z, me = ctx // PLANE, ctx % PLANE
    last = planes - 1
    groups = source.shape[0]
    half = groups // 2
    width = half * GROUP
    part = groups // CHUNKS
    f32, bf16 = jnp.float32, jnp.bfloat16

    def at(plane, place):
        return (plane * PLANE + place, ch)

    def remote(src, dst, send, recv, device):
        return pltpu.make_async_remote_copy(
            src_ref=src, dst_ref=dst, send_sem=send, recv_sem=recv,
            device_id=device, device_id_type=MESH)

    barrier = pltpu.get_barrier_semaphore()
    for step in range(1, PLANE):
        pl.semaphore_signal(barrier, inc=1, device_id=at(z, (me + step) % PLANE), device_id_type=MESH)

    @pl.when(z > 0)
    def _():
        for step in range(PLANE):
            pl.semaphore_signal(barrier, inc=1, device_id=at(z - 1, (me + step) % PLANE), device_id_type=MESH)

    for step in range(1, planes):
        @pl.when(z + step < planes)
        def _(step=step):
            pl.semaphore_signal(barrier, inc=1, device_id=at(z + step, me), device_id_type=MESH)

    loads = [
        pltpu.make_async_copy(k_hbm, k_v, load_sem.at[0]),
        pltpu.make_async_copy(v_hbm, v_v, load_sem.at[1]),
        pltpu.make_async_copy(taps_hbm, taps_in.at[me], load_sem.at[2]),
        pltpu.make_async_copy(skip_hbm.at[pl.ds(pl.multiple_of(me * groups * GROUP, 256), groups * GROUP)], skip_v, load_sem.at[3]),
    ]
    for load in loads:
        load.start()

    @pl.when(z == 0)
    def _():
        source[:, 0:LAGS - 1] = jnp.zeros((groups, LAGS - 1, GROUP, BLOCK), bf16)

    pl.semaphore_wait(barrier, PLANE - 1 + z + jnp.where(z < last, PLANE, 0))

    tap_copies = []
    for step in range(1, PLANE):
        copy = remote(taps_hbm, taps_in.at[me], tap_send, tap_recv, at(z, (me + step) % PLANE))
        copy.start()
        tap_copies.append(copy)

    for step in range(2, planes):
        @pl.when(z - step >= 0)
        def _(step=step):
            pl.semaphore_signal(credit, inc=1, device_id=at(z - step, me), device_id_type=MESH)

    loads[0].wait()
    loads[1].wait()
    own_copies = []
    local_copies = {}
    pieces = [pl.ds(chunk * part, part) for chunk in range(CHUNKS)]

    def mix(to, which):
        lanes = pl.ds(pl.multiple_of(to * groups * GROUP + which * width, width), width)
        m = (k_v[:, lanes].astype(f32) * v_v[:, lanes].astype(f32)).T
        mixed[to, pl.ds(which * half, half)] = m.astype(bf16).reshape(half, GROUP, BLOCK)

    def send_own(chunk):
        for to in places[:-1]:
            copy = remote(mixed.at[to, pieces[chunk]], source.at[pieces[chunk], LAGS - 1 + me], own_send, own_recv.at[chunk], at(z, to))
            copy.start()
            own_copies.append(copy)
        copy = pltpu.make_async_copy(mixed.at[me, pieces[chunk]], source.at[pieces[chunk], LAGS - 1 + me], local_sem.at[chunk])
        copy.start()
        local_copies[chunk] = copy

    def halo(to, chunk):
        return remote(mixed.at[to, pieces[chunk]], source.at[pieces[chunk], jnp.maximum(me - 1, 0)], halo_send.at[0], halo_recv.at[chunk],
                      at(jnp.minimum(z + 1, last), to))

    def send_halo(chunk):
        @pl.when((z < last) & (me > 0))
        def _():
            for to in places:
                halo(to, chunk).start()

    def forward(chunk):
        return remote(source.at[pieces[chunk], LAGS:LAGS + PLANE - 1], source.at[pieces[chunk], 0:LAGS - 1], halo_send.at[1],
                      halo_recv.at[chunk], at(jnp.minimum(z + 1, last), me))

    landed = mixed.at[0:PLANE - 1, pl.ds(0, part)]

    def wait_own(chunk):
        local_copies[chunk].wait()
        pltpu.make_async_copy(landed, landed, own_recv.at[chunk]).wait()

    def send_forward(chunk):
        wait_own(chunk)

        @pl.when(z < last)
        def _():
            forward(chunk).start()

    places = [(me + step) % PLANE for step in range(1, PLANE)] + [me]

    def run(stage):
        for what, which in stage:
            if what == "m":
                for to in places:
                    mix(to, which)
            if what == "o":
                send_own(which)
            if what == "h":
                send_halo(which)
            if what == "f":
                send_forward(which)
            if what in "xy":
                @pl.when(ch % 2 == (0 if what == "x" else 1))
                def _(which=which):
                    send_halo(which)

    run(PLAN[0])

    loads[2].wait()
    pltpu.make_async_copy(taps_in.at[0:PLANE - 1], taps_in.at[0:PLANE - 1], tap_recv).wait()
    taps_f[...] = taps_in[...].astype(f32).reshape(BLOCK, BLOCK).T
    taps_own[...] = taps_f[pl.ds(pl.multiple_of(me * groups, groups), groups), :].astype(bf16)

    def line(step):
        return remote(taps_own, taps_all.at[z], line_send, line_recv.at[z], at(jnp.clip(z + step, 0, last), me))

    for step in range(-last, 2):
        if step != 0:
            @pl.when((z + step >= 0) & (z + step <= last))
            def _(step=step):
                line(step).start()
    taps_all[z] = taps_own[...]
    run(PLAN[1])

    @pl.when(z < last - 1)
    def _():
        pl.semaphore_wait(credit, last - 1 - z)

    for step in range(2, planes):
        @pl.when(z + step <= last)
        def _(step=step):
            line(step).start()

    loads[3].wait()
    per = BLOCK // GROUP
    for piece in range(groups // per):
        row = skip_v[piece * BLOCK:(piece + 1) * BLOCK].reshape(1, BLOCK)
        skip_rows[piece * per:(piece + 1) * per] = jnp.broadcast_to(row, (BLOCK, BLOCK)).T.reshape(per, GROUP, BLOCK)

    run(PLAN[2])


    run(PLAN[3])

    u = lax.broadcasted_iota(jnp.int32, (BLOCK, BLOCK), 0)
    t = lax.broadcasted_iota(jnp.int32, (BLOCK, BLOCK), 1)
    reached = t >= u

    def turn(lag, g):
        row = taps_row[lag, pl.ds(g, 1), :]
        return pltpu.roll(jnp.broadcast_to(row, (BLOCK, BLOCK)), 0, 1, stride=1, stride_axis=0)

    def rows_of(lags):
        for lag in lags:
            @pl.when(z != lag)
            def _(lag=lag):
                pltpu.make_async_copy(taps_own, taps_own, line_recv.at[lag]).wait()
            taps_row[lag] = taps_all[lag].astype(f32)

    def build(lags, g):
        before = turn(lags[0] - 1, g) if lags[0] else jnp.zeros((BLOCK, BLOCK), f32)
        for lag in lags:
            turned = turn(lag, g)
            toeplitz[g, lag * BLOCK:(lag + 1) * BLOCK, :] = jnp.where(reached, turned, before).astype(bf16)
            before = turned

    early, late = range(0, LAGS // 2), range(LAGS // 2, LAGS)
    rows_of(early)

    @pl.loop(0, groups, unroll=2)
    def _(g):
        build(early, g)

    rows_of(late)

    back_copies = []
    for chunk in range(CHUNKS):
        rows = pl.ds(chunk * part, part)
        if ("f", chunk) not in sum(PLAN, ()):
            wait_own(chunk)

        @pl.when(z > 0)
        def _(chunk=chunk):
            pltpu.make_async_copy(landed, landed, halo_recv.at[chunk]).wait()

        @pl.loop(chunk * part, (chunk + 1) * part, unroll=part)
        def _(g):
            build(late, g)
            total = jnp.broadcast_to(skip_rows[g][None], (PLANE, GROUP, BLOCK)).reshape(BLOCK, BLOCK)
            total = total * source[g, LAGS - 1:LAGS - 1 + PLANE].reshape(BLOCK, BLOCK).astype(f32)
            windows = [source[g, LAGS - 1 - lag:LAGS - 1 - lag + PLANE].reshape(BLOCK, BLOCK) for lag in range(LAGS)]
            total = total + jnp.dot(jnp.concatenate(windows, axis=1), toeplitz[g], preferred_element_type=f32)
            result[:, g] = total.astype(bf16).reshape(PLANE, GROUP, BLOCK)

        for to in places[:-1]:
            copy = remote(result.at[to, rows], back.at[me, rows], back_send, back_recv, at(z, to))
            copy.start()
            back_copies.append(copy)
    home = pltpu.make_async_copy(result.at[me], back.at[me], local_sem.at[CHUNKS])
    home.start()
    home.wait()

    for copy in tap_copies + own_copies + back_copies:
        copy.wait_send()
    for step in range(1, planes):
        line(1).wait_send()

    @pl.when((z < last) & (me > 0))
    def _():
        for what, chunk in sum(PLAN, ()):
            if what in "hx":
                for _ in range(PLANE):
                    halo(me, chunk).wait_send()

    @pl.when(z < last)
    def _():
        for what, chunk in sum(PLAN, ()):
            if what == "f":
                forward(chunk).wait_send()

    pltpu.make_async_copy(back.at[0:PLANE - 1], back.at[0:PLANE - 1], back_recv).wait()


def gate(back_ref, q_ref, out_ref):
    for first in range(0, q_ref.shape[1], BLOCK):
        lanes = slice(first, first + BLOCK)
        turned = back_ref[lanes, :].astype(jnp.float32).T
        out_ref[:, lanes] = (q_ref[:, lanes].astype(jnp.float32) * turned).astype(jnp.bfloat16)


def solution(mesh):
    planes = mesh.shape["ctx"] // PLANE

    def per_device(query, key, value, filter_taps, skip):
        tokens, channels = query.shape
        groups = channels // GROUP // PLANE
        hbm = pl.BlockSpec(memory_space=pl.ANY)
        bf16, f32 = jnp.bfloat16, jnp.float32
        dma = pltpu.SemaphoreType.DMA
        back = pl.pallas_call(
            functools.partial(kernel, planes),
            out_shape=jax.ShapeDtypeStruct((PLANE, groups, GROUP, BLOCK), bf16),
            in_specs=[hbm] * 4,
            out_specs=hbm,
            scratch_shapes=[
                pltpu.VMEM((tokens, channels), bf16),
                pltpu.VMEM((tokens, channels), bf16),
                pltpu.VMEM((groups * GROUP,), f32),
                pltpu.VMEM((groups, GROUP, BLOCK), f32),
                pltpu.VMEM((PLANE, groups, GROUP, BLOCK), bf16),
                pltpu.VMEM((groups, LAGS - 1 + PLANE, GROUP, BLOCK), bf16),
                pltpu.VMEM((PLANE, BLOCK // PLANE, BLOCK), bf16),
                pltpu.VMEM((BLOCK, BLOCK), f32),
                pltpu.VMEM((groups, BLOCK), bf16),
                pltpu.VMEM((planes, groups, BLOCK), bf16),
                pltpu.VMEM((planes, groups, BLOCK), f32),
                pltpu.VMEM((groups, LAGS * BLOCK, BLOCK), bf16),
                pltpu.VMEM((PLANE, groups, GROUP, BLOCK), bf16),
                dma((4,)), dma((CHUNKS + 1,)),
                dma, dma, dma, dma((planes,)),
                pltpu.SemaphoreType.REGULAR,
                dma, dma((CHUNKS,)), dma((2,)), dma((CHUNKS,)), dma, dma,
            ],
            compiler_params=pltpu.CompilerParams(collective_id=0, has_side_effects=True),
        )(key, value, filter_taps, skip)
        steps = STEPS
        return pl.pallas_call(
            gate,
            grid=(steps,),
            out_shape=jax.ShapeDtypeStruct((tokens, channels), bf16),
            in_specs=[pl.BlockSpec((channels // steps, BLOCK), lambda i: (i, 0)), pl.BlockSpec((tokens, channels // steps), lambda i: (0, i))],
            out_specs=pl.BlockSpec((tokens, channels // steps), lambda i: (0, i)),
        )(back.reshape(channels, BLOCK), query)

    placed = (P("ctx", "ch"), P("ctx", "ch"), P("ctx", "ch"), P("ctx", "ch"), P("ch"))
    return jax.shard_map(per_device, mesh=mesh, in_specs=placed, out_specs=P("ctx", "ch"), check_vma=False)
```
